32 devices in a mesh: tm: 8 (over z, y), chan: 4 (over x, core).
Axes of the slice: x: 2, y: 2, z: 4, core: 2. Of those that a mesh axis runs over, the one named last changes fastest.
Arguments:
- tokens: bfloat16 [16384, 1024], P('tm', 'chan'), may hold values from -170 to 170
- w_query: bfloat16 [1024, 1024], P(None, 'chan'), may hold values from -0.1875 to 0.1875
- w_key: bfloat16 [1024, 1024], P(None, 'chan'), may hold values from -0.1875 to 0.1875
- w_value: bfloat16 [1024, 1024], P(None, 'chan'), may hold values from -0.1875 to 0.1875
- w_out: bfloat16 [1024, 1024], P('chan'), may hold values from -0.25 to 0.25
- pool_kernel: float32 [2, 27, 64], replicated, may hold values from -1.25 to 1.25
Outputs:
- block_out: bfloat16 [16384, 1024], P('tm', 'chan')
The draws below stay inside these ranges and needn't reach their ends.
All inputs are finite; a program needn't handle non-finite values.
Results may differ from the reference program's by a relative error of at most 0.0053.
Values may be sent and summed in bfloat16 or wider, within the bound.
A program may use at most 128 MiB of HBM per device.

```python
import math
import jax
import jax.numpy as jnp
from jax import lax

D = 1024
HEADS = 16
HDIM = 64
HH = 16
WW = 16
TOK_DEV = 2048
POOLED = 64
FRAMES = 64
TOKENS = 16384
N_TM = 8


def draw_tokens(key, part):
    first_key = jax.random.fold_in(key, 0)
    normal_draw = jax.random.normal(first_key, (TOKENS, D), jnp.float32)
    return jnp.clip(normal_draw, -6.0, 6.0).astype(jnp.bfloat16)


def spiked(values, key, source, target, parts, factor):
    def block_of(position):
        return (jnp.arange(values.shape[position]) // (values.shape[position] // parts)).reshape((-1,) + (1,) * (values.ndim - 1 - position))

    first = jax.random.permutation(key, parts)[block_of(target)]
    second = (block_of(target) + parts // 2) % parts
    return jnp.where((block_of(source) == first) | (block_of(source) == second), factor * values, values)


def shard_levels(rng, shape, pieces, smallest, high):
    level, own = 1.0, jax.random.fold_in(rng, 6)
    for position, blocks in pieces:
        heights = jnp.exp(jax.random.uniform(jax.random.fold_in(own, position), (blocks,), jnp.float32, smallest / len(pieces), high / len(pieces)))
        level = level * jnp.repeat(heights, shape[position] // blocks).reshape([-1 if axis == position else 1 for axis in range(len(shape))])
    return level


def bell_draw(stream_key, shape, deviation, bound, shards=(), kind=jnp.bfloat16):
    result = jax.random.normal(stream_key, shape, jnp.float32) * deviation
    if len(shards) > 0:
        result = shard_levels(stream_key, shape, shards, -0.22, 0.18) * result
    return jnp.clip(result, min=-bound, max=bound).astype(kind)


def noise_with(key, extent, scale, most, shards, heavy, held_as=jnp.bfloat16):
    drawn = scale * jax.random.normal(key, extent, jnp.float32)
    if shards:
        drawn = drawn * shard_levels(key, extent, shards, -0.22, 0.18)
    return jnp.clip(spiked(drawn, jax.random.fold_in(key, 3), *heavy), -most, most).astype(held_as)


def setup_inputs(seed: int = 0) -> dict:
    key_of = jax.random.split(jax.random.key(seed), 7)
    return {
        "tokens": draw_tokens(jax.random.fold_in(key_of[6], 71), 0),
        "w_query": bell_draw(key_of[1], (D, D), D ** -0.5, 0.1875, ((1, 4),)),
        "w_key": bell_draw(key_of[2], (D, D), D ** -0.5, 0.1875, ((1, 4),)),
        "w_value": bell_draw(key_of[3], (D, D), D ** -0.5, 0.1875, ((1, 4),)),
        "w_out": noise_with(key_of[4], (D, D), D ** -0.5, 0.25, ((0, 4),), (0, 1, 4, 2.0)),
        "pool_kernel": bell_draw(key_of[5], (2, 27, HDIM), 27 ** -0.5, 1.25, (), jnp.float32),
    }


epsilon = 1e-06

def head_norm(field, head_width):
    shape = field.shape
    split = field.reshape(shape[:-1] + (shape[-1] // head_width, head_width))
    center = split - lax.optimization_barrier(jnp.mean(split, axis=-1, keepdims=True))
    spread = lax.optimization_barrier(jnp.mean(center * center, axis=-1, keepdims=True))
    return (center * lax.rsqrt(spread + epsilon)).reshape(shape)

def pool_field(field, kernel):
    earlier = jnp.roll(field, 1, axis=0)
    sources = (earlier[0::2], field[0::2], field[1::2])
    running = jnp.zeros((field.shape[0] // 2, HH // 4, WW // 4, field.shape[3]), jnp.float32)
    for first in range(3):
        padded = jnp.pad(sources[first], ((0, 0), (1, 0), (1, 0), (0, 0)))
        for second in range(3):
            for third in range(3):
                picked = padded[:, second:second + HH:4, third:third + WW:4, :]
                running = running + picked * kernel[9 * first + 3 * second + third]
    return running

def reference(tokens, w_query, w_key, w_value, w_out, pool_kernel):
    reach = min(6, (N_TM - 1) // 2)
    key_all = jnp.dot(tokens, w_key, preferred_element_type=jnp.float32).astype(jnp.bfloat16)
    value_all = jnp.dot(tokens, w_value, preferred_element_type=jnp.float32).astype(jnp.bfloat16)
    kernel_k = jnp.tile(pool_kernel[0], (1, HEADS))
    kernel_v = jnp.tile(pool_kernel[1], (1, HEADS))
    pooled_k = pool_field(key_all.astype(jnp.float32).reshape(FRAMES, HH, WW, D), kernel_k)
    pooled_k = head_norm(pooled_k, HDIM).astype(jnp.bfloat16).reshape(N_TM, POOLED, D)
    pooled_v = pool_field(value_all.astype(jnp.float32).reshape(FRAMES, HH, WW, D), kernel_v)
    pooled_v = head_norm(pooled_v, HDIM).astype(jnp.bfloat16).reshape(N_TM, POOLED, D)

    def one_block(index):
        rows_here = lax.dynamic_slice_in_dim(tokens, (index * TOK_DEV).astype(jnp.int32), TOK_DEV, 0)
        queries = jnp.dot(rows_here, w_query, preferred_element_type=jnp.float32).astype(jnp.bfloat16)
        chosen = (index + jnp.arange(-reach, reach + 1, dtype=jnp.int32)) % N_TM
        key_rows = pooled_k[chosen].reshape(-1, HEADS, HDIM).astype(jnp.float32)
        value_rows = pooled_v[chosen].reshape(-1, HEADS, HDIM).astype(jnp.float32)
        query_heads = queries.astype(jnp.float32).reshape(TOK_DEV, HEADS, HDIM)
        scores = jnp.einsum('qhd,khd->hqk', query_heads, key_rows) / math.sqrt(HDIM)
        highest = lax.optimization_barrier(jnp.max(scores, axis=-1, keepdims=True))
        weighted = jnp.exp(scores - highest)
        summed = lax.optimization_barrier(jnp.sum(weighted, axis=-1))
        weights_bf = weighted.astype(jnp.bfloat16).astype(jnp.float32)
        blended = jnp.einsum('hqk,khd->qhd', weights_bf, value_rows)
        attended = (blended / summed.T[:, :, None] + query_heads).astype(jnp.bfloat16).reshape(TOK_DEV, D)
        projected = jnp.dot(attended, w_out, preferred_element_type=jnp.float32)
        return (rows_here.astype(jnp.float32) + projected).astype(jnp.bfloat16)
    return lax.map(one_block, jnp.arange(N_TM, dtype=jnp.int32)).reshape(TOKENS, D)
```

```python
import functools

import jax
import jax.numpy as jnp
from jax import lax
from jax.experimental import pallas as pl
from jax.experimental.pallas import tpu as pltpu
from jax.sharding import PartitionSpec as P

D = 1024
HEADS = 16
HDIM = 64
HH = 16
WW = 16
FRAME = HH * WW
EPSILON = 1e-06
MESH = pl.DeviceIdType.MESH
HIGHEST = lax.Precision.HIGHEST
f32 = jnp.float32
bf16 = jnp.bfloat16


def kernel(
    n_tm, reach, frames, width,
    tokens, w_query, w_key, w_value, w_out, pool_kernel, out,
    tok, weights, wo, queries, field, taps, pre, halo_out, halo_in, gathered, k_big, v_big, att,
    local_sem, tok_send, tok_recv, wo_send, wo_recv, halo_send, halo_recv,
    gat_send, gat_recv, att_send, att_recv,
):
    tm = lax.axis_index("tm")
    me = lax.axis_index("chan")
    sib = me + 1 - 2 * lax.rem(me, 2)
    across = lax.rem(me + 2, 4)
    diag = lax.rem(sib + 2, 4)
    heads = width // HDIM
    pairs = frames // 2
    offsets = [d for d in range(-reach, reach + 1) if d != 0]

    def tm_at(d):
        return lax.rem(tm + d + n_tm, n_tm)

    def rows_of(frame):
        return pl.ds(pl.multiple_of(frame * FRAME, FRAME), FRAME)

    loads = [
        pltpu.make_async_copy(w_query, weights.at[:, pl.ds(0, width)], local_sem.at[0]),
        pltpu.make_async_copy(w_key, weights.at[:, pl.ds(width, width)], local_sem.at[1]),
        pltpu.make_async_copy(w_value, weights.at[:, pl.ds(2 * width, width)], local_sem.at[2]),
        pltpu.make_async_copy(tokens, tok.at[me], local_sem.at[3]),
        pltpu.make_async_copy(
            w_out.at[:, pl.ds(pl.multiple_of(me * width, width), width)], wo.at[me], local_sem.at[4]
        ),
    ]
    for load in loads:
        load.start()

    barrier = pltpu.get_barrier_semaphore()
    for other in (sib, across, diag):
        pl.semaphore_signal(barrier, inc=1, device_id={"chan": other}, device_id_type=MESH)
    for d in offsets:
        pl.semaphore_signal(barrier, inc=1, device_id={"tm": tm_at(d)}, device_id_type=MESH)
    pl.semaphore_wait(barrier, 3 + len(offsets))

    def token_copy(kind, frame):
        rows = rows_of(frame)
        if kind == 2:
            source, slot = tok.at[across, rows], across
        else:
            source, slot = tokens.at[rows], me
        return pltpu.make_async_remote_copy(
            src_ref=source, dst_ref=tok.at[slot, rows],
            send_sem=tok_send.at[kind, frame], recv_sem=tok_recv.at[kind, frame],
            device_id={"chan": across if kind == 0 else sib}, device_id_type=MESH,
        )

    def token_arrival(kind, frame):
        rows = rows_of(frame)
        slot = (across, sib, diag)[kind]
        return pltpu.make_async_remote_copy(
            src_ref=tok.at[slot, rows], dst_ref=tok.at[slot, rows],
            send_sem=tok_send.at[kind, frame], recv_sem=tok_recv.at[kind, frame],
            device_id={"chan": across if kind == 0 else sib}, device_id_type=MESH,
        )

    def att_copy(kind, frame):
        rows = rows_of(frame)
        slot = across if kind == 2 else me
        return pltpu.make_async_remote_copy(
            src_ref=att.at[slot, rows], dst_ref=att.at[slot, rows],
            send_sem=att_send.at[kind, frame], recv_sem=att_recv.at[kind, frame],
            device_id={"chan": across if kind == 0 else sib}, device_id_type=MESH,
        )

    def att_arrival(kind, frame):
        rows = rows_of(frame)
        slot = (across, sib, diag)[kind]
        return pltpu.make_async_remote_copy(
            src_ref=att.at[slot, rows], dst_ref=att.at[slot, rows],
            send_sem=att_send.at[kind, frame], recv_sem=att_recv.at[kind, frame],
            device_id={"chan": across if kind == 0 else sib}, device_id_type=MESH,
        )

    def pair_at(step):
        return lax.rem(step + pairs - 1, pairs)

    @pl.loop(0, pairs)
    def _(step):
        for second in range(2):
            frame = 2 * pair_at(step) + second
            token_copy(0, frame).start()
            token_copy(1, frame).start()

    wo_copies = []
    for index, other in enumerate((sib, across, diag)):
        copy = pltpu.make_async_remote_copy(
            src_ref=w_out.at[:, pl.ds(pl.multiple_of(other * width, width), width)],
            dst_ref=wo.at[me], send_sem=wo_send.at[index], recv_sem=wo_recv.at[index],
            device_id={"chan": other}, device_id_type=MESH,
        )
        copy.start()
        wo_copies.append(copy)

    channel = lax.broadcasted_iota(jnp.int32, (HDIM, 2 * width), 1)
    inner = lax.broadcasted_iota(jnp.int32, (HDIM, 2 * width), 0)
    same = lax.rem(channel, HDIM) == inner
    spread_k = (same & (channel < width)).astype(f32)
    spread_v = (same & (channel >= width)).astype(f32)
    wide = jnp.dot(pool_kernel[0], spread_k, precision=HIGHEST, preferred_element_type=f32)
    wide = wide + jnp.dot(pool_kernel[1], spread_v, precision=HIGHEST, preferred_element_type=f32)
    column = lax.broadcasted_iota(jnp.int32, (WW, 2 * width), 0)
    place = lax.rem(column, 4)
    for tap in range(9):
        line = jnp.where((place == 3) & (column < WW - 1), wide[3 * tap : 3 * tap + 1], 0.0)
        line = jnp.where(place == 0, wide[3 * tap + 1 : 3 * tap + 2], line)
        line = jnp.where(place == 1, wide[3 * tap + 2 : 3 * tap + 3], line)
        taps[tap] = line
    pre[...] = jnp.zeros_like(pre)

    def slab(slot, first, i):
        total = None
        for second in range(3):
            row = 4 * i - 1 + second
            if row < 0:
                continue
            term = field[slot, row] * taps[3 * first + second]
            total = term if total is None else total + term
        return total

    def column_sum(block):
        rows_in = block.shape[0]
        r = lax.broadcasted_iota(jnp.int32, (rows_in // 4, rows_in), 0)
        c = lax.broadcasted_iota(jnp.int32, (rows_in // 4, rows_in), 1)
        pick = ((c >= 4 * r - 1) & (c <= 4 * r + 1)).astype(f32)
        return jnp.dot(pick, block, precision=HIGHEST, preferred_element_type=f32)

    halo = pltpu.make_async_remote_copy(
        src_ref=halo_out, dst_ref=halo_in, send_sem=halo_send, recv_sem=halo_recv,
        device_id={"tm": tm_at(1)}, device_id_type=MESH,
    )

    for load in loads[:4]:
        load.wait()

    @pl.loop(0, pairs)
    def _(step):
        pair = pair_at(step)
        for second in range(2):
            frame = 2 * pair + second
            token_arrival(0, frame).wait_recv()
            token_copy(2, frame).start()
        for second in range(2):
            frame = 2 * pair + second
            rows = rows_of(frame)
            token_arrival(1, frame).wait_recv()
            token_arrival(2, frame).wait_recv()
            total = None
            for s in range(4):
                term = jnp.dot(
                    tok[s, rows], weights[s * width : (s + 1) * width, :], preferred_element_type=f32
                )
                total = term if total is None else total + term
            total = total.astype(bf16)
            queries[rows, :] = total[:, :width]
            field[second] = total[:, width:].astype(f32).reshape(HH, WW, 2 * width)
        for i in range(HH // 4):
            pre[pair, i] = pre[pair, i] + slab(0, 1, i) + slab(1, 2, i)
            pre[pair + 1, i] = pre[pair + 1, i] + slab(1, 0, i)

        @pl.when(step == 0)
        def _():
            halo_out[...] = column_sum(pre[pairs].reshape(HH // 4 * WW, 2 * width))
            halo.start()

    pooled = column_sum(pre[0:pairs].reshape(pairs * HH // 4 * WW, 2 * width))
    halo.wait_recv()
    block_rows = pooled.shape[0]
    halo_rows = HH // 4 * (WW // 4)
    pooled = jnp.concatenate([pooled[:halo_rows] + halo_in[...], pooled[halo_rows:]], axis=0)
    g0 = lax.broadcasted_iota(jnp.int32, (width, width), 0) // HDIM
    g1 = lax.broadcasted_iota(jnp.int32, (width, width), 1) // HDIM
    averaging = jnp.where(g0 == g1, 1.0 / HDIM, 0.0).astype(f32)
    for part in range(2):
        x = pooled[:, part * width : (part + 1) * width]
        center = x - jnp.dot(x, averaging, precision=HIGHEST, preferred_element_type=f32)
        spread = jnp.dot(center * center, averaging, precision=HIGHEST, preferred_element_type=f32)
        gathered[reach, :, part * width : (part + 1) * width] = (
            center * lax.rsqrt(spread + EPSILON)
        ).astype(bf16)

    sends = []
    for index, d in enumerate(offsets):
        copy = pltpu.make_async_remote_copy(
            src_ref=gathered.at[reach], dst_ref=gathered.at[reach - d],
            send_sem=gat_send.at[index], recv_sem=gat_recv.at[reach - d],
            device_id={"tm": tm_at(d)}, device_id_type=MESH,
        )
        copy.start()
        sends.append(copy)

    lane_head = lax.broadcasted_iota(jnp.int32, (block_rows, width), 1) // HDIM

    def spread_block(slot):
        rows = slice(slot * block_rows, (slot + 1) * block_rows)
        keys = gathered[slot, :, :width]
        values = gathered[slot, :, width:]
        for h in range(heads):
            k_big[h, rows, :] = keys * jnp.where(lane_head == h, HDIM**-0.5, 0.0).astype(bf16)
            v_big[h, rows, :] = values * jnp.where(lane_head == h, 1.0, 0.0).astype(bf16)

    spread_block(reach)
    for index, d in enumerate(offsets):
        slot = reach + d
        pltpu.make_async_remote_copy(
            src_ref=gathered.at[reach], dst_ref=gathered.at[slot],
            send_sem=gat_send.at[index], recv_sem=gat_recv.at[slot],
            device_id={"tm": tm_at(d)}, device_id_type=MESH,
        ).wait_recv()
        spread_block(slot)

    out_head = lax.broadcasted_iota(jnp.int32, (FRAME, width), 1) // HDIM

    @pl.loop(0, frames)
    def _(frame):
        rows = rows_of(frame)
        q = queries[rows, :]
        blended = None
        divisor = None
        for h in range(heads):
            scores = lax.dot_general(
                q, k_big[h], (((1,), (1,)), ((), ())), preferred_element_type=f32
            )
            weighted = jnp.exp(scores - jnp.max(scores, axis=-1, keepdims=True))
            summed = jnp.sum(weighted, axis=-1, keepdims=True)
            term = jnp.dot(weighted.astype(bf16), v_big[h], preferred_element_type=f32)
            blended = term if blended is None else blended + term
            wide_sum = jnp.broadcast_to(summed, (FRAME, width))
            divisor = wide_sum if divisor is None else jnp.where(out_head == h, wide_sum, divisor)
        att[me, rows] = (blended / divisor + q.astype(f32)).astype(bf16)
        att_copy(0, frame).start()
        att_copy(1, frame).start()

    loads[4].wait()
    for index, other in enumerate((sib, across, diag)):
        pltpu.make_async_remote_copy(
            src_ref=wo.at[other], dst_ref=wo.at[other],
            send_sem=wo_send.at[index], recv_sem=wo_recv.at[index],
            device_id={"chan": other}, device_id_type=MESH,
        ).wait_recv()

    @pl.loop(0, frames)
    def _(frame):
        rows = rows_of(frame)
        att_arrival(0, frame).wait_recv()
        att_copy(2, frame).start()
        att_arrival(1, frame).wait_recv()
        att_arrival(2, frame).wait_recv()
        total = tok[me, rows].astype(f32)
        for s in range(4):
            total = total + jnp.dot(att[s, rows], wo[s], preferred_element_type=f32)
        out[rows, :] = total.astype(bf16)

    @pl.loop(0, frames)
    def _(frame):
        for kind in range(3):
            token_copy(kind, frame).wait_send()
            att_copy(kind, frame).wait_send()

    for copy in wo_copies + sends + [halo]:
        copy.wait_send()


def per_device(n_tm, n_chan, tokens, w_query, w_key, w_value, w_out, pool_kernel):
    rows, width = tokens.shape
    frames = rows // FRAME
    pairs = frames // 2
    block = pairs * (HH // 4) * (WW // 4)
    reach = min(6, (n_tm - 1) // 2)
    spans = 2 * reach + 1
    heads = width // HDIM
    dma = pltpu.SemaphoreType.DMA
    anywhere = pl.BlockSpec(memory_space=pl.ANY)
    vmem = pl.BlockSpec(memory_space=pltpu.VMEM)
    return pl.pallas_call(
        functools.partial(kernel, n_tm, reach, frames, width),
        out_shape=jax.ShapeDtypeStruct((rows, width), bf16),
        in_specs=[anywhere] * 5 + [vmem],
        out_specs=vmem,
        scratch_shapes=[
            pltpu.VMEM((n_chan, rows, width), bf16),
            pltpu.VMEM((D, 3 * width), bf16),
            pltpu.VMEM((n_chan, width, width), bf16),
            pltpu.VMEM((rows, width), bf16),
            pltpu.VMEM((2, HH, WW, 2 * width), f32),
            pltpu.VMEM((9, WW, 2 * width), f32),
            pltpu.VMEM((pairs + 1, HH // 4, WW, 2 * width), f32),
            pltpu.VMEM((HH // 4 * (WW // 4), 2 * width), f32),
            pltpu.VMEM((HH // 4 * (WW // 4), 2 * width), f32),
            pltpu.VMEM((spans, block, 2 * width), bf16),
            pltpu.VMEM((heads, spans * block, width), bf16),
            pltpu.VMEM((heads, spans * block, width), bf16),
            pltpu.VMEM((n_chan, rows, width), bf16),
            dma((5,)),
            dma((3, frames)),
            dma((3, frames)),
            dma((3,)),
            dma((3,)),
            dma,
            dma,
            dma((2 * reach,)),
            dma((spans,)),
            dma((3, frames)),
            dma((3, frames)),
        ],
        compiler_params=pltpu.CompilerParams(
            collective_id=0, has_side_effects=True, vmem_limit_bytes=48 * 1024 * 1024
        ),
    )(tokens, w_query, w_key, w_value, w_out, pool_kernel)


def solution(mesh):
    shape = dict(mesh.shape)
    return jax.shard_map(
        functools.partial(per_device, shape["tm"], shape["chan"]),
        mesh=mesh,
        in_specs=(
            P("tm", "chan"),
            P(None, "chan"),
            P(None, "chan"),
            P(None, "chan"),
            P("chan", None),
            P(),
        ),
        out_specs=P("tm", "chan"),
        check_vma=False,
    )
```

```python
import functools

import jax
import jax.numpy as jnp
from jax import lax
from jax.experimental import pallas as pl
from jax.experimental.pallas import tpu as pltpu
from jax.sharding import PartitionSpec as P

D = 1024
HEADS = 16
HDIM = 64
HH = 16
WW = 16
FRAME = HH * WW
EPSILON = 1e-06
MESH = pl.DeviceIdType.MESH
HIGHEST = lax.Precision.HIGHEST
f32 = jnp.float32
bf16 = jnp.bfloat16


def kernel(
    n_tm, reach, frames, width,
    tokens, w_query, w_key, w_value, w_out, pool_hbm, out,
    pool_kernel, tok, weights, wo, queries, field, taps, pre, halo_out, halo_in, gathered, k_big, v_big, att,
    local_sem, tok_send, tok_recv, wo_send, wo_recv, halo_send, halo_recv,
    gat_send, gat_recv, att_send, att_recv,
):
    tm = lax.axis_index("tm")
    me = lax.axis_index("chan")
    sib = me + 1 - 2 * lax.rem(me, 2)
    across = lax.rem(me + 2, 4)
    diag = lax.rem(sib + 2, 4)
    heads = width // HDIM
    pairs = frames // 2
    relayed = n_tm == 8
    beside = tm + 1 - 2 * lax.rem(tm, 2)
    offsets = [-2, -1, 1, 2, 4] if relayed else [d for d in range(-reach, reach + 1) if d != 0]

    def tm_at(d):
        return lax.rem(tm + d + n_tm, n_tm)

    def rows_of(frame):
        return pl.ds(pl.multiple_of(frame * FRAME, FRAME), FRAME)

    loads = [
        pltpu.make_async_copy(w_query, weights.at[:, pl.ds(0, width)], local_sem.at[0]),
        pltpu.make_async_copy(w_key, weights.at[:, pl.ds(width, width)], local_sem.at[1]),
        pltpu.make_async_copy(w_value, weights.at[:, pl.ds(2 * width, width)], local_sem.at[2]),
        pltpu.make_async_copy(tokens, tok.at[me], local_sem.at[3]),
        pltpu.make_async_copy(
            w_out.at[:, pl.ds(pl.multiple_of(me * width, width), width)], wo.at[me], local_sem.at[4]
        ),
        pltpu.make_async_copy(pool_hbm, pool_kernel, local_sem.at[5]),
    ]
    for load in loads:
        load.start()

    barrier = pltpu.get_barrier_semaphore()
    for other in (sib, across, diag):
        pl.semaphore_signal(barrier, inc=1, device_id={"chan": other}, device_id_type=MESH)
    for d in offsets:
        pl.semaphore_signal(barrier, inc=1, device_id={"tm": tm_at(d)}, device_id_type=MESH)
    pl.semaphore_wait(barrier, 3 + len(offsets))

    def part_of(ref, pair, part):
        both = pl.ds(2 * pair, 2)
        if part == 0:
            return ref.at[both, :, pl.ds(0, 2)]
        if part == 1:
            return ref.at[both, pl.ds(0, 3), 3]
        if part == 2:
            return ref.at[both, :, 2]
        return ref.at[both, 3, 3]

    def token_copy(kind, pair, part):
        if kind == 2:
            source, slot = part_of(tok.at[across], pair, part), across
        else:
            source, slot = part_of(tokens, pair, part), me
        return pltpu.make_async_remote_copy(
            src_ref=source, dst_ref=part_of(tok.at[slot], pair, part),
            send_sem=tok_send.at[kind, pair, part], recv_sem=tok_recv.at[kind, pair, part],
            device_id={"chan": across if kind == 0 else sib}, device_id_type=MESH,
        )

    def token_arrival(kind, pair, part):
        place = part_of(tok.at[(across, sib, diag)[kind]], pair, part)
        return pltpu.make_async_remote_copy(
            src_ref=place, dst_ref=place,
            send_sem=tok_send.at[kind, pair, part], recv_sem=tok_recv.at[kind, pair, part],
            device_id={"chan": across if kind == 0 else sib}, device_id_type=MESH,
        )

    def att_copy(kind, frame):
        rows = rows_of(frame)
        slot = across if kind == 2 else me
        return pltpu.make_async_remote_copy(
            src_ref=att.at[slot, rows], dst_ref=att.at[slot, rows],
            send_sem=att_send.at[kind, frame], recv_sem=att_recv.at[kind, frame],
            device_id={"chan": across if kind == 0 else sib}, device_id_type=MESH,
        )

    def att_arrival(kind, frame):
        rows = rows_of(frame)
        slot = (across, sib, diag)[kind]
        return pltpu.make_async_remote_copy(
            src_ref=att.at[slot, rows], dst_ref=att.at[slot, rows],
            send_sem=att_send.at[kind, frame], recv_sem=att_recv.at[kind, frame],
            device_id={"chan": across if kind == 0 else sib}, device_id_type=MESH,
        )

    def pair_at(step):
        return lax.rem(step + pairs - 1, pairs)

    for parts in ((0, 1), (2, 3)):
        @pl.loop(0, pairs)
        def _(step, parts=parts):
            for part in parts:
                token_copy(0, pair_at(step), part).start()
                token_copy(1, pair_at(step), part).start()

    wo_copies = []
    for index, other in enumerate((sib, across, diag)):
        copy = pltpu.make_async_remote_copy(
            src_ref=w_out.at[:, pl.ds(pl.multiple_of(other * width, width), width)],
            dst_ref=wo.at[me], send_sem=wo_send.at[index], recv_sem=wo_recv.at[index],
            device_id={"chan": other}, device_id_type=MESH,
        )
        copy.start()
        wo_copies.append(copy)

    loads[5].wait()
    channel = lax.broadcasted_iota(jnp.int32, (HDIM, 2 * width), 1)
    inner = lax.broadcasted_iota(jnp.int32, (HDIM, 2 * width), 0)
    same = lax.rem(channel, HDIM) == inner
    spread_k = (same & (channel < width)).astype(f32)
    spread_v = (same & (channel >= width)).astype(f32)
    wide = jnp.dot(pool_kernel[0], spread_k, precision=HIGHEST, preferred_element_type=f32)
    wide = wide + jnp.dot(pool_kernel[1], spread_v, precision=HIGHEST, preferred_element_type=f32)
    column = lax.broadcasted_iota(jnp.int32, (WW, 2 * width), 0)
    place = lax.rem(column, 4)
    for tap in range(9):
        line = jnp.where((place == 3) & (column < WW - 1), wide[3 * tap : 3 * tap + 1], 0.0)
        line = jnp.where(place == 0, wide[3 * tap + 1 : 3 * tap + 2], line)
        line = jnp.where(place == 1, wide[3 * tap + 2 : 3 * tap + 3], line)
        taps[tap] = line
    pre[...] = jnp.zeros_like(pre)

    def slab(slot, first, i):
        total = None
        for second in range(3):
            if i == 0 and second == 0:
                continue
            group, row = (i - 1, 3) if second == 0 else (i, second - 1)
            term = field[slot, group, row] * taps[3 * first + second]
            total = term if total is None else total + term
        return total

    def column_sum(block):
        rows_in = block.shape[0]
        r = lax.broadcasted_iota(jnp.int32, (rows_in // 4, rows_in), 0)
        c = lax.broadcasted_iota(jnp.int32, (rows_in // 4, rows_in), 1)
        pick = ((c >= 4 * r - 1) & (c <= 4 * r + 1)).astype(f32)
        return jnp.dot(pick, block, precision=HIGHEST, preferred_element_type=f32)

    halo = pltpu.make_async_remote_copy(
        src_ref=halo_out, dst_ref=halo_in, send_sem=halo_send, recv_sem=halo_recv,
        device_id={"tm": tm_at(1)}, device_id_type=MESH,
    )

    for load in loads[:4]:
        load.wait()

    def project(pair, parts, columns):
        arrivals = []
        for part in parts:
            token_arrival(0, pair, part).wait_recv()
            token_copy(2, pair, part).start()
        for part in parts:
            token_arrival(1, pair, part).wait_recv()
            token_arrival(2, pair, part).wait_recv()
        total = None
        for s in range(4):
            pieces = [part_of(tok.at[s], pair, part)[...].reshape(-1, width) for part in parts]
            term = jnp.dot(
                jnp.concatenate(pieces, axis=0),
                weights[s * width : (s + 1) * width, :columns],
                preferred_element_type=f32,
            )
            total = term if total is None else total + term
        return total.astype(bf16)

    def project_pooled(pair):
        total = project(pair, (0, 1), 3 * width)
        both = pl.ds(2 * pair, 2)
        queries[both, :, 0:2] = total[:FRAME, :width].reshape(2, 4, 2, WW, width)
        queries[both, 0:3, 3] = total[FRAME:, :width].reshape(2, 3, WW, width)
        field[:, :, 0:2] = total[:FRAME, width:].astype(f32).reshape(2, 4, 2, WW, 2 * width)
        field[:, 0:3, 3] = total[FRAME:, width:].astype(f32).reshape(2, 3, WW, 2 * width)
        for i in range(HH // 4):
            pre[pair, i] = pre[pair, i] + slab(0, 1, i) + slab(1, 2, i)
            pre[pair + 1, i] = pre[pair + 1, i] + slab(1, 0, i)

    g0 = lax.broadcasted_iota(jnp.int32, (width, width), 0) // HDIM
    g1 = lax.broadcasted_iota(jnp.int32, (width, width), 1) // HDIM
    averaging = jnp.where(g0 == g1, 1.0 / HDIM, 0.0).astype(f32)
    half = pairs // 2
    halo_rows = HH // 4 * (WW // 4)
    half_rows = half * halo_rows

    def normalise(phase):
        pooled = column_sum(
            pre[phase * half : (phase + 1) * half].reshape(half * HH // 4 * WW, 2 * width)
        )
        if phase == 0:
            pooled = jnp.concatenate([pooled[:halo_rows] + halo_in[...], pooled[halo_rows:]], axis=0)
        for part in range(2):
            x = pooled[:, part * width : (part + 1) * width]
            center = x - jnp.dot(x, averaging, precision=HIGHEST, preferred_element_type=f32)
            spread = jnp.dot(
                center * center, averaging, precision=HIGHEST, preferred_element_type=f32
            )
            gathered[tm, phase, :, part * width : (part + 1) * width] = (
                center * lax.rsqrt(spread + EPSILON)
            ).astype(bf16)

    def block_copy(index, source, target, phase):
        return pltpu.make_async_remote_copy(
            src_ref=gathered.at[source, phase], dst_ref=gathered.at[source, phase],
            send_sem=gat_send.at[index, phase], recv_sem=gat_recv.at[source, phase],
            device_id={"tm": target}, device_id_type=MESH,
        )

    sends = []

    def send_block(phase):
        if relayed:
            targets = [tm_at(2), tm_at(6), tm_at(4), beside]
        else:
            targets = [tm_at(d) for d in offsets]
        for index, target in enumerate(targets):
            copy = block_copy(index, tm, target, phase)
            copy.start()
            sends.append(copy)

    def relay_block(phase):
        if not relayed:
            return
        for index, d in enumerate((2, 6, 4)):
            copy = block_copy(4 + index, tm_at(d), beside, phase)
            copy.wait_recv()
            copy.start()
            sends.append(copy)

    lane_head = lax.broadcasted_iota(jnp.int32, (half_rows, width), 1) // HDIM

    def spread_block(place, slot, phase):
        start = (2 * place + phase) * half_rows
        rows = slice(start, start + half_rows)
        keys = gathered[slot, phase, :, :width]
        values = gathered[slot, phase, :, width:]
        for h in range(heads):
            k_big[h, rows, :] = keys * jnp.where(lane_head == h, HDIM**-0.5, 0.0).astype(bf16)
            v_big[h, rows, :] = values * jnp.where(lane_head == h, 1.0, 0.0).astype(bf16)

    def spread_blocks(phase):
        spread_block(0, tm, phase)
        if relayed:
            for place, d in enumerate((2, 6)):
                spread_block(1 + place, tm_at(d), phase)
            others = [beside] + [lax.rem(beside + d, n_tm) for d in (2, 6, 4)]
            first = 3
        else:
            others = [tm_at(d) for d in offsets]
            first = 1
        for place, slot in enumerate(others):
            block_copy(0, slot, beside, phase).wait_recv()
            spread_block(first + place, slot, phase)

    project_pooled(pairs - 1)
    halo_out[...] = column_sum(pre[pairs].reshape(HH // 4 * WW, 2 * width))
    halo.start()

    @pl.loop(1, pairs - 1)
    def _(step):
        project_pooled(pair_at(step))

    halo.wait_recv()
    normalise(0)
    send_block(0)
    relay_block(0)
    project_pooled(pairs - 2)
    normalise(1)
    send_block(1)
    spread_blocks(0)
    relay_block(1)

    @pl.loop(0, pairs)
    def _(step):
        pair = pair_at(step)
        total = project(pair, (2, 3), width)
        both = pl.ds(2 * pair, 2)
        queries[both, :, 2] = total[: FRAME // 2].reshape(2, 4, WW, width)
        queries[both, 3, 3] = total[FRAME // 2 :].reshape(2, WW, width)

    spread_blocks(1)

    out_head = lax.broadcasted_iota(jnp.int32, (FRAME, width), 1) // HDIM

    @pl.loop(0, frames)
    def _(frame):
        rows = rows_of(frame)
        q = queries[frame].reshape(FRAME, width)
        blended = None
        divisor = None
        for h in range(heads):
            scores = lax.dot_general(
                q, k_big[h], (((1,), (1,)), ((), ())), preferred_element_type=f32
            )
            weighted = jnp.exp(scores - jnp.max(scores, axis=-1, keepdims=True))
            summed = jnp.sum(weighted, axis=-1, keepdims=True)
            term = jnp.dot(weighted.astype(bf16), v_big[h], preferred_element_type=f32)
            blended = term if blended is None else blended + term
            wide_sum = jnp.broadcast_to(summed, (FRAME, width))
            divisor = wide_sum if divisor is None else jnp.where(out_head == h, wide_sum, divisor)
        att[me, rows] = (blended / divisor + q.astype(f32)).astype(bf16)
        att_copy(0, frame).start()
        att_copy(1, frame).start()

    loads[4].wait()
    for index, other in enumerate((sib, across, diag)):
        pltpu.make_async_remote_copy(
            src_ref=wo.at[other], dst_ref=wo.at[other],
            send_sem=wo_send.at[index], recv_sem=wo_recv.at[index],
            device_id={"chan": other}, device_id_type=MESH,
        ).wait_recv()

    @pl.loop(0, frames)
    def _(frame):
        rows = rows_of(frame)
        att_arrival(0, frame).wait_recv()
        att_copy(2, frame).start()
        att_arrival(1, frame).wait_recv()
        att_arrival(2, frame).wait_recv()
        total = tok[me, frame].reshape(FRAME, width).astype(f32)
        for s in range(4):
            total = total + jnp.dot(att[s, rows], wo[s], preferred_element_type=f32)
        out[rows, :] = total.astype(bf16)

    @pl.loop(0, frames)
    def _(frame):
        for kind in range(3):
            att_copy(kind, frame).wait_send()

    @pl.loop(0, pairs)
    def _(pair):
        for kind in range(3):
            for part in range(4):
                token_copy(kind, pair, part).wait_send()

    for copy in wo_copies + sends + [halo]:
        copy.wait_send()


def per_device(n_tm, n_chan, tokens, w_query, w_key, w_value, w_out, pool_kernel):
    rows, width = tokens.shape
    frames = rows // FRAME
    pairs = frames // 2
    block = pairs * (HH // 4) * (WW // 4)
    reach = min(6, (n_tm - 1) // 2)
    spans = 2 * reach + 1
    heads = width // HDIM
    dma = pltpu.SemaphoreType.DMA
    anywhere = pl.BlockSpec(memory_space=pltpu.HBM)
    vmem = pl.BlockSpec(memory_space=pltpu.VMEM)
    return pl.pallas_call(
        functools.partial(kernel, n_tm, reach, frames, width),
        out_shape=jax.ShapeDtypeStruct((rows, width), bf16),
        in_specs=[anywhere] * 6,
        out_specs=vmem,
        scratch_shapes=[
            pltpu.VMEM(pool_kernel.shape, f32),
            pltpu.VMEM((n_chan, frames, HH // 4, 4, WW, width), bf16),
            pltpu.VMEM((D, 3 * width), bf16),
            pltpu.VMEM((n_chan, width, width), bf16),
            pltpu.VMEM((frames, HH // 4, 4, WW, width), bf16),
            pltpu.VMEM((2, HH // 4, 4, WW, 2 * width), f32),
            pltpu.VMEM((9, WW, 2 * width), f32),
            pltpu.VMEM((pairs + 1, HH // 4, WW, 2 * width), f32),
            pltpu.VMEM((HH // 4 * (WW // 4), 2 * width), f32),
            pltpu.VMEM((HH // 4 * (WW // 4), 2 * width), f32),
            pltpu.VMEM((n_tm, 2, block // 2, 2 * width), bf16),
            pltpu.VMEM((heads, spans * block, width), bf16),
            pltpu.VMEM((heads, spans * block, width), bf16),
            pltpu.VMEM((n_chan, rows, width), bf16),
            dma((6,)),
            dma((3, pairs, 4)),
            dma((3, pairs, 4)),
            dma((3,)),
            dma((3,)),
            dma,
            dma,
            dma((max(7, 2 * reach), 2)),
            dma((n_tm, 2)),
            dma((3, frames)),
            dma((3, frames)),
        ],
        compiler_params=pltpu.CompilerParams(
            collective_id=0, has_side_effects=True, vmem_limit_bytes=63 * 1024 * 1024
        ),
    )(tokens.reshape(frames, HH // 4, 4, WW, width), w_query, w_key, w_value, w_out, pool_kernel)


def solution(mesh):
    shape = dict(mesh.shape)
    return jax.shard_map(
        functools.partial(per_device, shape["tm"], shape["chan"]),
        mesh=mesh,
        in_specs=(
            P("tm", "chan"),
            P(None, "chan"),
            P(None, "chan"),
            P(None, "chan"),
            P("chan", None),
            P(),
        ),
        out_specs=P("tm", "chan"),
        check_vma=False,
    )
```

```python
import functools

import jax
import jax.numpy as jnp
from jax import lax
from jax.experimental import pallas as pl
from jax.experimental.pallas import tpu as pltpu
from jax.sharding import PartitionSpec as P

D = 1024
HEADS = 16
HDIM = 64
HH = 16
WW = 16
FRAME = HH * WW
EPSILON = 1e-06
MESH = pl.DeviceIdType.MESH
HIGHEST = lax.Precision.HIGHEST
f32 = jnp.float32
bf16 = jnp.bfloat16


def kernel(
    n_tm, reach, frames, width,
    tokens, w_query, w_key, w_value, w_out, pool_hbm, out,
    pool_kernel, tok, weights, wo, queries, field, taps, pre, halo_out, halo_in, gathered, k_big, v_big, att,
    local_sem, tok_send, tok_recv, wo_send, wo_recv, halo_send, halo_recv,
    gat_send, gat_recv, att_send, att_recv,
):
    tm = lax.axis_index("tm")
    me = lax.axis_index("chan")
    sib = me + 1 - 2 * lax.rem(me, 2)
    across = lax.rem(me + 2, 4)
    diag = lax.rem(sib + 2, 4)
    heads = width // HDIM
    pairs = frames // 2
    relayed = n_tm == 8
    beside = tm + 1 - 2 * lax.rem(tm, 2)
    offsets = [-2, -1, 1, 2, 4] if relayed else [d for d in range(-reach, reach + 1) if d != 0]

    def tm_at(d):
        return lax.rem(tm + d + n_tm, n_tm)

    def rows_of(frame):
        return pl.ds(pl.multiple_of(frame * FRAME, FRAME), FRAME)

    loads = [
        pltpu.make_async_copy(w_query, weights.at[:, pl.ds(0, width)], local_sem.at[0]),
        pltpu.make_async_copy(w_key, weights.at[:, pl.ds(width, width)], local_sem.at[1]),
        pltpu.make_async_copy(w_value, weights.at[:, pl.ds(2 * width, width)], local_sem.at[2]),
        pltpu.make_async_copy(
            w_out.at[:, pl.ds(pl.multiple_of(me * width, width), width)], wo.at[me], local_sem.at[4]
        ),
        pltpu.make_async_copy(pool_hbm, pool_kernel, local_sem.at[3]),
    ] + [
        pltpu.make_async_copy(tokens.at[:, :, :, row], tok.at[me, :, kept], local_sem.at[5 + kept])
        for kept, row in enumerate((0, 1, 3, 2))
    ]
    for load in loads:
        load.start()

    barrier = pltpu.get_barrier_semaphore()
    for other in (sib, across, diag):
        pl.semaphore_signal(barrier, inc=1, device_id={"chan": other}, device_id_type=MESH)
    for d in offsets:
        pl.semaphore_signal(barrier, inc=1, device_id={"tm": tm_at(d)}, device_id_type=MESH)
    pl.semaphore_wait(barrier, 3 + len(offsets))

    def part_of(ref, pair, part):
        return ref.at[pair, pl.ds(0, 3)] if part == 0 else ref.at[pair, 3]

    def token_copy(kind, pair, part):
        if kind == 2:
            source, slot = part_of(tok.at[across], pair, part), across
        else:
            source, slot = part_of(tok.at[me], pair, part), me
        return pltpu.make_async_remote_copy(
            src_ref=source, dst_ref=part_of(tok.at[slot], pair, part),
            send_sem=tok_send.at[kind, pair, part], recv_sem=tok_recv.at[kind, pair, part],
            device_id={"chan": across if kind == 0 else sib}, device_id_type=MESH,
        )

    def token_arrival(kind, pair, part):
        place = part_of(tok.at[(across, sib, diag)[kind]], pair, part)
        return pltpu.make_async_remote_copy(
            src_ref=place, dst_ref=place,
            send_sem=tok_send.at[kind, pair, part], recv_sem=tok_recv.at[kind, pair, part],
            device_id={"chan": across if kind == 0 else sib}, device_id_type=MESH,
        )

    def att_copy(kind, frame):
        rows = rows_of(frame)
        slot = across if kind == 2 else me
        return pltpu.make_async_remote_copy(
            src_ref=att.at[slot, rows], dst_ref=att.at[slot, rows],
            send_sem=att_send.at[kind, frame], recv_sem=att_recv.at[kind, frame],
            device_id={"chan": across if kind == 0 else sib}, device_id_type=MESH,
        )

    def att_arrival(kind, frame):
        rows = rows_of(frame)
        slot = (across, sib, diag)[kind]
        return pltpu.make_async_remote_copy(
            src_ref=att.at[slot, rows], dst_ref=att.at[slot, rows],
            send_sem=att_send.at[kind, frame], recv_sem=att_recv.at[kind, frame],
            device_id={"chan": across if kind == 0 else sib}, device_id_type=MESH,
        )

    def pair_at(step):
        return lax.rem(step + pairs - 1, pairs)

    for load in loads[5:]:
        load.wait()
    for parts in ((0,), (1,)):
        @pl.loop(0, pairs)
        def _(step, parts=parts):
            for part in parts:
                token_copy(0, pair_at(step), part).start()
                token_copy(1, pair_at(step), part).start()

    wo_copies = []
    for index, other in enumerate((sib, across, diag)):
        copy = pltpu.make_async_remote_copy(
            src_ref=w_out.at[:, pl.ds(pl.multiple_of(other * width, width), width)],
            dst_ref=wo.at[me], send_sem=wo_send.at[index], recv_sem=wo_recv.at[index],
            device_id={"chan": other}, device_id_type=MESH,
        )
        copy.start()
        wo_copies.append(copy)

    loads[4].wait()
    channel = lax.broadcasted_iota(jnp.int32, (HDIM, 2 * width), 1)
    inner = lax.broadcasted_iota(jnp.int32, (HDIM, 2 * width), 0)
    same = lax.rem(channel, HDIM) == inner
    spread_k = (same & (channel < width)).astype(f32)
    spread_v = (same & (channel >= width)).astype(f32)
    wide = jnp.dot(pool_kernel[0], spread_k, precision=HIGHEST, preferred_element_type=f32)
    wide = wide + jnp.dot(pool_kernel[1], spread_v, precision=HIGHEST, preferred_element_type=f32)
    column = lax.broadcasted_iota(jnp.int32, (WW, 2 * width), 0)
    place = lax.rem(column, 4)
    for tap in range(9):
        line = jnp.where((place == 3) & (column < WW - 1), wide[3 * tap : 3 * tap + 1], 0.0)
        line = jnp.where(place == 0, wide[3 * tap + 1 : 3 * tap + 2], line)
        line = jnp.where(place == 1, wide[3 * tap + 2 : 3 * tap + 3], line)
        taps[tap] = line
    pre[...] = jnp.zeros_like(pre)

    def slab(slot, first, i):
        total = None
        for second in range(3):
            if i == 0 and second == 0:
                continue
            group, row = (i - 1, 3) if second == 0 else (i, second - 1)
            term = field[slot, group, row] * taps[3 * first + second]
            total = term if total is None else total + term
        return total

    def column_sum(block):
        rows_in = block.shape[0]
        r = lax.broadcasted_iota(jnp.int32, (rows_in // 4, rows_in), 0)
        c = lax.broadcasted_iota(jnp.int32, (rows_in // 4, rows_in), 1)
        pick = ((c >= 4 * r - 1) & (c <= 4 * r + 1)).astype(f32)
        return jnp.dot(pick, block, precision=HIGHEST, preferred_element_type=f32)

    halo = pltpu.make_async_remote_copy(
        src_ref=halo_out, dst_ref=halo_in, send_sem=halo_send, recv_sem=halo_recv,
        device_id={"tm": tm_at(1)}, device_id_type=MESH,
    )

    for load in loads[:3]:
        load.wait()

    def project(pair, parts, columns):
        arrivals = []
        for part in parts:
            token_arrival(0, pair, part).wait_recv()
            token_copy(2, pair, part).start()
        for part in parts:
            token_arrival(1, pair, part).wait_recv()
            token_arrival(2, pair, part).wait_recv()
        total = None
        for s in range(4):
            pieces = [part_of(tok.at[s], pair, part)[...].reshape(-1, width) for part in parts]
            term = jnp.dot(
                jnp.concatenate(pieces, axis=0),
                weights[s * width : (s + 1) * width, :columns],
                preferred_element_type=f32,
            )
            total = term if total is None else total + term
        return total.astype(bf16)

    def project_pooled(pair):
        total = project(pair, (0,), 3 * width)
        both = pl.ds(2 * pair, 2)
        for kept, row in enumerate((0, 1, 3)):
            block = total[kept * FRAME // 2 : (kept + 1) * FRAME // 2]
            queries[both, :, row] = block[:, :width].reshape(2, 4, WW, width)
            field[:, :, row] = block[:, width:].astype(f32).reshape(2, 4, WW, 2 * width)
        for i in range(HH // 4):
            pre[pair, i] = pre[pair, i] + slab(0, 1, i) + slab(1, 2, i)
            pre[pair + 1, i] = pre[pair + 1, i] + slab(1, 0, i)

    g0 = lax.broadcasted_iota(jnp.int32, (width, width), 0) // HDIM
    g1 = lax.broadcasted_iota(jnp.int32, (width, width), 1) // HDIM
    averaging = jnp.where(g0 == g1, 1.0 / HDIM, 0.0).astype(f32)
    half = pairs // 2
    halo_rows = HH // 4 * (WW // 4)
    half_rows = half * halo_rows

    def normalise(phase):
        pooled = column_sum(
            pre[phase * half : (phase + 1) * half].reshape(half * HH // 4 * WW, 2 * width)
        )
        if phase == 0:
            pooled = jnp.concatenate([pooled[:halo_rows] + halo_in[...], pooled[halo_rows:]], axis=0)
        for part in range(2):
            x = pooled[:, part * width : (part + 1) * width]
            center = x - jnp.dot(x, averaging, precision=HIGHEST, preferred_element_type=f32)
            spread = jnp.dot(
                center * center, averaging, precision=HIGHEST, preferred_element_type=f32
            )
            gathered[tm, phase, :, part * width : (part + 1) * width] = (
                center * lax.rsqrt(spread + EPSILON)
            ).astype(bf16)

    def block_copy(index, source, target, phase):
        return pltpu.make_async_remote_copy(
            src_ref=gathered.at[source, phase], dst_ref=gathered.at[source, phase],
            send_sem=gat_send.at[index, phase], recv_sem=gat_recv.at[source, phase],
            device_id={"tm": target}, device_id_type=MESH,
        )

    sends = []

    def send_block(phase):
        if relayed:
            targets = [tm_at(2), tm_at(6), tm_at(4), beside]
        else:
            targets = [tm_at(d) for d in offsets]
        for index, target in enumerate(targets):
            copy = block_copy(index, tm, target, phase)
            copy.start()
            sends.append(copy)

    def relay_block(phase):
        if not relayed:
            return
        for index, d in enumerate((2, 6, 4)):
            copy = block_copy(4 + index, tm_at(d), beside, phase)
            copy.wait_recv()
            copy.start()
            sends.append(copy)

    lane_head = lax.broadcasted_iota(jnp.int32, (half_rows, width), 1) // HDIM

    def spread_block(place, slot, phase):
        start = (2 * place + phase) * half_rows
        rows = slice(start, start + half_rows)
        keys = gathered[slot, phase, :, :width]
        values = gathered[slot, phase, :, width:]
        for h in range(heads):
            k_big[h, rows, :] = keys * jnp.where(lane_head == h, HDIM**-0.5, 0.0).astype(bf16)
            v_big[h, rows, :] = values * jnp.where(lane_head == h, 1.0, 0.0).astype(bf16)

    def spread_blocks(phase):
        spread_block(0, tm, phase)
        if relayed:
            for place, d in enumerate((2, 6)):
                spread_block(1 + place, tm_at(d), phase)
            others = [beside] + [lax.rem(beside + d, n_tm) for d in (2, 6, 4)]
            first = 3
        else:
            others = [tm_at(d) for d in offsets]
            first = 1
        for place, slot in enumerate(others):
            block_copy(0, slot, beside, phase).wait_recv()
            spread_block(first + place, slot, phase)

    project_pooled(pairs - 1)
    halo_out[...] = column_sum(pre[pairs].reshape(HH // 4 * WW, 2 * width))
    halo.start()

    @pl.loop(1, pairs - 1)
    def _(step):
        project_pooled(pair_at(step))

    halo.wait_recv()
    normalise(0)
    send_block(0)
    relay_block(0)
    project_pooled(pairs - 2)
    normalise(1)
    send_block(1)
    spread_blocks(0)
    relay_block(1)

    @pl.loop(0, pairs)
    def _(step):
        pair = pair_at(step)
        total = project(pair, (1,), width)
        both = pl.ds(2 * pair, 2)
        queries[both, :, 2] = total.reshape(2, 4, WW, width)

    spread_blocks(1)

    out_head = lax.broadcasted_iota(jnp.int32, (FRAME, width), 1) // HDIM

    @pl.loop(0, frames)
    def _(frame):
        rows = rows_of(frame)
        q = queries[frame].reshape(FRAME, width)
        blended = None
        divisor = None
        for h in range(heads):
            scores = lax.dot_general(
                q, k_big[h], (((1,), (1,)), ((), ())), preferred_element_type=f32
            )
            weighted = jnp.exp(scores - jnp.max(scores, axis=-1, keepdims=True))
            summed = jnp.sum(weighted, axis=-1, keepdims=True)
            term = jnp.dot(weighted.astype(bf16), v_big[h], preferred_element_type=f32)
            blended = term if blended is None else blended + term
            wide_sum = jnp.broadcast_to(summed, (FRAME, width))
            divisor = wide_sum if divisor is None else jnp.where(out_head == h, wide_sum, divisor)
        att[me, rows] = (blended / divisor + q.astype(f32)).astype(bf16)
        att_copy(0, frame).start()
        att_copy(1, frame).start()

    loads[3].wait()
    for index, other in enumerate((sib, across, diag)):
        pltpu.make_async_remote_copy(
            src_ref=wo.at[other], dst_ref=wo.at[other],
            send_sem=wo_send.at[index], recv_sem=wo_recv.at[index],
            device_id={"chan": other}, device_id_type=MESH,
        ).wait_recv()

    @pl.loop(0, frames)
    def _(frame):
        rows = rows_of(frame)
        att_arrival(0, frame).wait_recv()
        att_copy(2, frame).start()
        att_arrival(1, frame).wait_recv()
        att_arrival(2, frame).wait_recv()
        own = [tok[me, frame // 2, kept, lax.rem(frame, 2)] for kept in (0, 1, 3, 2)]
        total = jnp.stack(own, axis=1).reshape(FRAME, width).astype(f32)
        for s in range(4):
            total = total + jnp.dot(att[s, rows], wo[s], preferred_element_type=f32)
        out[rows, :] = total.astype(bf16)

    @pl.loop(0, frames)
    def _(frame):
        for kind in range(3):
            att_copy(kind, frame).wait_send()

    @pl.loop(0, pairs)
    def _(pair):
        for kind in range(3):
            for part in range(2):
                token_copy(kind, pair, part).wait_send()

    for copy in wo_copies + sends + [halo]:
        copy.wait_send()


def per_device(n_tm, n_chan, tokens, w_query, w_key, w_value, w_out, pool_kernel):
    rows, width = tokens.shape
    frames = rows // FRAME
    pairs = frames // 2
    block = pairs * (HH // 4) * (WW // 4)
    reach = min(6, (n_tm - 1) // 2)
    spans = 2 * reach + 1
    heads = width // HDIM
    dma = pltpu.SemaphoreType.DMA
    anywhere = pl.BlockSpec(memory_space=pltpu.HBM)
    vmem = pl.BlockSpec(memory_space=pltpu.VMEM)
    return pl.pallas_call(
        functools.partial(kernel, n_tm, reach, frames, width),
        out_shape=jax.ShapeDtypeStruct((rows, width), bf16),
        in_specs=[anywhere] * 6,
        out_specs=vmem,
        scratch_shapes=[
            pltpu.VMEM(pool_kernel.shape, f32),
            pltpu.VMEM((n_chan, pairs, 4, 2, HH // 4, WW, width), bf16),
            pltpu.VMEM((D, 3 * width), bf16),
            pltpu.VMEM((n_chan, width, width), bf16),
            pltpu.VMEM((frames, HH // 4, 4, WW, width), bf16),
            pltpu.VMEM((2, HH // 4, 4, WW, 2 * width), f32),
            pltpu.VMEM((9, WW, 2 * width), f32),
            pltpu.VMEM((pairs + 1, HH // 4, WW, 2 * width), f32),
            pltpu.VMEM((HH // 4 * (WW // 4), 2 * width), f32),
            pltpu.VMEM((HH // 4 * (WW // 4), 2 * width), f32),
            pltpu.VMEM((n_tm, 2, block // 2, 2 * width), bf16),
            pltpu.VMEM((heads, spans * block, width), bf16),
            pltpu.VMEM((heads, spans * block, width), bf16),
            pltpu.VMEM((n_chan, rows, width), bf16),
            dma((9,)),
            dma((3, pairs, 2)),
            dma((3, pairs, 2)),
            dma((3,)),
            dma((3,)),
            dma,
            dma,
            dma((max(7, 2 * reach), 2)),
            dma((n_tm, 2)),
            dma((3, frames)),
            dma((3, frames)),
        ],
        compiler_params=pltpu.CompilerParams(
            collective_id=0, has_side_effects=True, vmem_limit_bytes=63 * 1024 * 1024
        ),
    )(tokens.reshape(pairs, 2, HH // 4, 4, WW, width), w_query, w_key, w_value, w_out, pool_kernel)


def solution(mesh):
    shape = dict(mesh.shape)
    return jax.shard_map(
        functools.partial(per_device, shape["tm"], shape["chan"]),
        mesh=mesh,
        in_specs=(
            P("tm", "chan"),
            P(None, "chan"),
            P(None, "chan"),
            P(None, "chan"),
            P("chan", None),
            P(),
        ),
        out_specs=P("tm", "chan"),
        check_vma=False,
    )
```

```python
import functools

import jax
import jax.numpy as jnp
from jax import lax
from jax.experimental import pallas as pl
from jax.experimental.pallas import tpu as pltpu
from jax.sharding import PartitionSpec as P

D = 1024
HEADS = 16
HDIM = 64
HH = 16
WW = 16
FRAME = HH * WW
EPSILON = 1e-06
MESH = pl.DeviceIdType.MESH
HIGHEST = lax.Precision.HIGHEST
f32 = jnp.float32
bf16 = jnp.bfloat16


def kernel(
    n_tm, reach, frames, width,
    tokens, w_query, w_key, w_value, w_out, pool_hbm, out,
    pool_kernel, tok, weights, wo, queries, field, taps, pre, halo_out, halo_in, gathered, k_big, v_big, att,
    local_sem, tok_send, tok_recv, wo_send, wo_recv, halo_send, halo_recv,
    gat_send, gat_recv, att_send, att_recv,
):
    tm = lax.axis_index("tm")
    me = lax.axis_index("chan")
    sib = me + 1 - 2 * lax.rem(me, 2)
    across = lax.rem(me + 2, 4)
    diag = lax.rem(sib + 2, 4)
    heads = width // HDIM
    pairs = frames // 2
    relayed = n_tm == 8
    beside = tm + 1 - 2 * lax.rem(tm, 2)
    offsets = [-2, -1, 1, 2, 4] if relayed else [d for d in range(-reach, reach + 1) if d != 0]

    def tm_at(d):
        return lax.rem(tm + d + n_tm, n_tm)

    def rows_of(frame):
        return pl.ds(pl.multiple_of(frame * FRAME, FRAME), FRAME)

    loads = [
        pltpu.make_async_copy(w_query, weights.at[:, pl.ds(0, width)], local_sem.at[0]),
        pltpu.make_async_copy(w_key, weights.at[:, pl.ds(width, width)], local_sem.at[1]),
        pltpu.make_async_copy(w_value, weights.at[:, pl.ds(2 * width, width)], local_sem.at[2]),
        pltpu.make_async_copy(
            w_out.at[:, pl.ds(pl.multiple_of(me * width, width), width)], wo.at[me], local_sem.at[4]
        ),
        pltpu.make_async_copy(pool_hbm, pool_kernel, local_sem.at[3]),
    ] + [
        pltpu.make_async_copy(tokens.at[:, :, :, row], tok.at[me, :, kept], local_sem.at[5 + kept])
        for kept, row in enumerate((0, 1, 3, 2))
    ]
    for load in loads:
        load.start()

    barrier = pltpu.get_barrier_semaphore()
    for other in (sib, across, diag):
        pl.semaphore_signal(barrier, inc=1, device_id={"chan": other}, device_id_type=MESH)
    for d in offsets:
        pl.semaphore_signal(barrier, inc=1, device_id={"tm": tm_at(d)}, device_id_type=MESH)
    pl.semaphore_wait(barrier, 3 + len(offsets))

    def part_of(ref, pair, part):
        return ref.at[pair, pl.ds(0, 3)] if part == 0 else ref.at[pair, 3]

    def token_copy(kind, pair, part):
        if kind == 2:
            source, slot = part_of(tok.at[across], pair, part), across
        else:
            source, slot = part_of(tok.at[me], pair, part), me
        return pltpu.make_async_remote_copy(
            src_ref=source, dst_ref=part_of(tok.at[slot], pair, part),
            send_sem=tok_send.at[kind, pair, part], recv_sem=tok_recv.at[kind, pair, part],
            device_id={"chan": across if kind == 0 else sib}, device_id_type=MESH,
        )

    def token_arrival(kind, pair, part):
        place = part_of(tok.at[(across, sib, diag)[kind]], pair, part)
        return pltpu.make_async_remote_copy(
            src_ref=place, dst_ref=place,
            send_sem=tok_send.at[kind, pair, part], recv_sem=tok_recv.at[kind, pair, part],
            device_id={"chan": across if kind == 0 else sib}, device_id_type=MESH,
        )

    def att_copy(kind, frame):
        rows = rows_of(frame)
        slot = across if kind == 2 else me
        return pltpu.make_async_remote_copy(
            src_ref=att.at[slot, rows], dst_ref=att.at[slot, rows],
            send_sem=att_send.at[kind, frame], recv_sem=att_recv.at[kind, frame],
            device_id={"chan": across if kind == 0 else sib}, device_id_type=MESH,
        )

    def att_arrival(kind, frame):
        rows = rows_of(frame)
        slot = (across, sib, diag)[kind]
        return pltpu.make_async_remote_copy(
            src_ref=att.at[slot, rows], dst_ref=att.at[slot, rows],
            send_sem=att_send.at[kind, frame], recv_sem=att_recv.at[kind, frame],
            device_id={"chan": across if kind == 0 else sib}, device_id_type=MESH,
        )

    def pair_at(step):
        return lax.rem(step + pairs - 1, pairs)

    for load in loads[5:]:
        load.wait()
    for parts in ((0,), (1,)):
        @pl.loop(0, pairs)
        def _(step, parts=parts):
            for part in parts:
                token_copy(0, pair_at(step), part).start()

    for part in range(2):
        @pl.loop(0, pairs)
        def _(step, part=part):
            token_copy(1, pair_at(step), part).start()

    wo_copies = []
    for index, other in enumerate((sib, across, diag)):
        copy = pltpu.make_async_remote_copy(
            src_ref=w_out.at[:, pl.ds(pl.multiple_of(other * width, width), width)],
            dst_ref=wo.at[me], send_sem=wo_send.at[index], recv_sem=wo_recv.at[index],
            device_id={"chan": other}, device_id_type=MESH,
        )
        copy.start()
        wo_copies.append(copy)

    loads[4].wait()
    channel = lax.broadcasted_iota(jnp.int32, (HDIM, 2 * width), 1)
    inner = lax.broadcasted_iota(jnp.int32, (HDIM, 2 * width), 0)
    same = lax.rem(channel, HDIM) == inner
    spread_k = (same & (channel < width)).astype(f32)
    spread_v = (same & (channel >= width)).astype(f32)
    wide = jnp.dot(pool_kernel[0], spread_k, precision=HIGHEST, preferred_element_type=f32)
    wide = wide + jnp.dot(pool_kernel[1], spread_v, precision=HIGHEST, preferred_element_type=f32)
    column = lax.broadcasted_iota(jnp.int32, (WW, 2 * width), 0)
    place = lax.rem(column, 4)
    for tap in range(9):
        line = jnp.where((place == 3) & (column < WW - 1), wide[3 * tap : 3 * tap + 1], 0.0)
        line = jnp.where(place == 0, wide[3 * tap + 1 : 3 * tap + 2], line)
        line = jnp.where(place == 1, wide[3 * tap + 2 : 3 * tap + 3], line)
        taps[tap] = line
    pre[...] = jnp.zeros_like(pre)

    def slab(slot, first, i):
        total = None
        for second in range(3):
            if i == 0 and second == 0:
                continue
            group, row = (i - 1, 3) if second == 0 else (i, second - 1)
            term = field[slot, group, row] * taps[3 * first + second]
            total = term if total is None else total + term
        return total

    def column_sum(block):
        rows_in = block.shape[0]
        r = lax.broadcasted_iota(jnp.int32, (rows_in // 4, rows_in), 0)
        c = lax.broadcasted_iota(jnp.int32, (rows_in // 4, rows_in), 1)
        pick = ((c >= 4 * r - 1) & (c <= 4 * r + 1)).astype(f32)
        return jnp.dot(pick, block, precision=HIGHEST, preferred_element_type=f32)

    halo = pltpu.make_async_remote_copy(
        src_ref=halo_out, dst_ref=halo_in, send_sem=halo_send, recv_sem=halo_recv,
        device_id={"tm": tm_at(1)}, device_id_type=MESH,
    )

    for load in loads[:3]:
        load.wait()

    def project(pair, parts, columns):
        arrivals = []
        for part in parts:
            token_arrival(0, pair, part).wait_recv()
            token_copy(2, pair, part).start()
        for part in parts:
            token_arrival(1, pair, part).wait_recv()
            token_arrival(2, pair, part).wait_recv()
        total = None
        for s in range(4):
            pieces = [part_of(tok.at[s], pair, part)[...].reshape(-1, width) for part in parts]
            term = jnp.dot(
                jnp.concatenate(pieces, axis=0),
                weights[s * width : (s + 1) * width, :columns],
                preferred_element_type=f32,
            )
            total = term if total is None else total + term
        return total.astype(bf16)

    def project_pooled(pair):
        total = project(pair, (0,), 3 * width)
        both = pl.ds(2 * pair, 2)
        for kept, row in enumerate((0, 1, 3)):
            block = total[kept * FRAME // 2 : (kept + 1) * FRAME // 2]
            queries[both, :, row] = block[:, :width].reshape(2, 4, WW, width)
            field[:, :, row] = block[:, width:].astype(f32).reshape(2, 4, WW, 2 * width)
        for i in range(HH // 4):
            pre[pair, i] = pre[pair, i] + slab(0, 1, i) + slab(1, 2, i)
            pre[pair + 1, i] = pre[pair + 1, i] + slab(1, 0, i)

    g0 = lax.broadcasted_iota(jnp.int32, (width, width), 0) // HDIM
    g1 = lax.broadcasted_iota(jnp.int32, (width, width), 1) // HDIM
    averaging = jnp.where(g0 == g1, 1.0 / HDIM, 0.0).astype(f32)
    half = pairs // 2
    halo_rows = HH // 4 * (WW // 4)
    half_rows = half * halo_rows

    def normalise(phase):
        pooled = column_sum(
            pre[phase * half : (phase + 1) * half].reshape(half * HH // 4 * WW, 2 * width)
        )
        if phase == 0:
            pooled = jnp.concatenate([pooled[:halo_rows] + halo_in[...], pooled[halo_rows:]], axis=0)
        for part in range(2):
            x = pooled[:, part * width : (part + 1) * width]
            center = x - jnp.dot(x, averaging, precision=HIGHEST, preferred_element_type=f32)
            spread = jnp.dot(
                center * center, averaging, precision=HIGHEST, preferred_element_type=f32
            )
            gathered[tm, phase, :, part * width : (part + 1) * width] = (
                center * lax.rsqrt(spread + EPSILON)
            ).astype(bf16)

    def block_copy(index, source, target, phase):
        return pltpu.make_async_remote_copy(
            src_ref=gathered.at[source, phase], dst_ref=gathered.at[source, phase],
            send_sem=gat_send.at[index, phase], recv_sem=gat_recv.at[source, phase],
            device_id={"tm": target}, device_id_type=MESH,
        )

    sends = []

    def send_block(phase):
        if relayed:
            targets = [tm_at(2), tm_at(6), tm_at(4), beside]
        else:
            targets = [tm_at(d) for d in offsets]
        for index, target in enumerate(targets):
            copy = block_copy(index, tm, target, phase)
            copy.start()
            sends.append(copy)

    def relay_block(phase):
        if not relayed:
            return
        for index, d in enumerate((2, 6, 4)):
            copy = block_copy(4 + index, tm_at(d), beside, phase)
            copy.wait_recv()
            copy.start()
            sends.append(copy)

    lane_head = lax.broadcasted_iota(jnp.int32, (half_rows, width), 1) // HDIM

    def spread_block(place, slot, phase):
        start = (2 * place + phase) * half_rows
        rows = slice(start, start + half_rows)
        keys = gathered[slot, phase, :, :width]
        values = gathered[slot, phase, :, width:]
        for h in range(heads):
            k_big[h, rows, :] = keys * jnp.where(lane_head == h, HDIM**-0.5, 0.0).astype(bf16)
            v_big[h, rows, :] = values * jnp.where(lane_head == h, 1.0, 0.0).astype(bf16)

    def spread_blocks(phase):
        spread_block(0, tm, phase)
        if relayed:
            for place, d in enumerate((2, 6)):
                spread_block(1 + place, tm_at(d), phase)
            others = [beside] + [lax.rem(beside + d, n_tm) for d in (2, 6, 4)]
            first = 3
        else:
            others = [tm_at(d) for d in offsets]
            first = 1
        for place, slot in enumerate(others):
            block_copy(0, slot, beside, phase).wait_recv()
            spread_block(first + place, slot, phase)

    project_pooled(pairs - 1)
    halo_out[...] = column_sum(pre[pairs].reshape(HH // 4 * WW, 2 * width))
    halo.start()

    @pl.loop(1, pairs - 1)
    def _(step):
        project_pooled(pair_at(step))

    halo.wait_recv()
    normalise(0)
    send_block(0)
    relay_block(0)
    project_pooled(pairs - 2)
    normalise(1)
    send_block(1)
    spread_blocks(0)
    relay_block(1)

    @pl.loop(0, pairs)
    def _(step):
        pair = pair_at(step)
        total = project(pair, (1,), width)
        both = pl.ds(2 * pair, 2)
        queries[both, :, 2] = total.reshape(2, 4, WW, width)

    spread_blocks(1)

    out_head = lax.broadcasted_iota(jnp.int32, (FRAME, width), 1) // HDIM

    @pl.loop(0, frames)
    def _(frame):
        rows = rows_of(frame)
        q = queries[frame].reshape(FRAME, width)
        blended = None
        divisor = None
        for h in range(heads):
            scores = lax.dot_general(
                q, k_big[h], (((1,), (1,)), ((), ())), preferred_element_type=f32
            )
            weighted = jnp.exp(scores - jnp.max(scores, axis=-1, keepdims=True))
            summed = jnp.sum(weighted, axis=-1, keepdims=True)
            term = jnp.dot(weighted.astype(bf16), v_big[h], preferred_element_type=f32)
            blended = term if blended is None else blended + term
            wide_sum = jnp.broadcast_to(summed, (FRAME, width))
            divisor = wide_sum if divisor is None else jnp.where(out_head == h, wide_sum, divisor)
        att[me, rows] = (blended / divisor + q.astype(f32)).astype(bf16)
        att_copy(0, frame).start()
        att_copy(1, frame).start()

    loads[3].wait()
    for index, other in enumerate((sib, across, diag)):
        pltpu.make_async_remote_copy(
            src_ref=wo.at[other], dst_ref=wo.at[other],
            send_sem=wo_send.at[index], recv_sem=wo_recv.at[index],
            device_id={"chan": other}, device_id_type=MESH,
        ).wait_recv()

    @pl.loop(0, frames)
    def _(frame):
        rows = rows_of(frame)
        att_arrival(0, frame).wait_recv()
        att_copy(2, frame).start()
        att_arrival(1, frame).wait_recv()
        att_arrival(2, frame).wait_recv()
        own = [tok[me, frame // 2, kept, lax.rem(frame, 2)] for kept in (0, 1, 3, 2)]
        total = jnp.stack(own, axis=1).reshape(FRAME, width).astype(f32)
        for s in range(4):
            total = total + jnp.dot(att[s, rows], wo[s], preferred_element_type=f32)
        out[rows, :] = total.astype(bf16)

    @pl.loop(0, frames)
    def _(frame):
        for kind in range(3):
            att_copy(kind, frame).wait_send()

    @pl.loop(0, pairs)
    def _(pair):
        for kind in range(3):
            for part in range(2):
                token_copy(kind, pair, part).wait_send()

    for copy in wo_copies + sends + [halo]:
        copy.wait_send()


def per_device(n_tm, n_chan, tokens, w_query, w_key, w_value, w_out, pool_kernel):
    rows, width = tokens.shape
    frames = rows // FRAME
    pairs = frames // 2
    block = pairs * (HH // 4) * (WW // 4)
    reach = min(6, (n_tm - 1) // 2)
    spans = 2 * reach + 1
    heads = width // HDIM
    dma = pltpu.SemaphoreType.DMA
    anywhere = pl.BlockSpec(memory_space=pltpu.HBM)
    vmem = pl.BlockSpec(memory_space=pltpu.VMEM)
    return pl.pallas_call(
        functools.partial(kernel, n_tm, reach, frames, width),
        out_shape=jax.ShapeDtypeStruct((rows, width), bf16),
        in_specs=[anywhere] * 6,
        out_specs=vmem,
        scratch_shapes=[
            pltpu.VMEM(pool_kernel.shape, f32),
            pltpu.VMEM((n_chan, pairs, 4, 2, HH // 4, WW, width), bf16),
            pltpu.VMEM((D, 3 * width), bf16),
            pltpu.VMEM((n_chan, width, width), bf16),
            pltpu.VMEM((frames, HH // 4, 4, WW, width), bf16),
            pltpu.VMEM((2, HH // 4, 4, WW, 2 * width), f32),
            pltpu.VMEM((9, WW, 2 * width), f32),
            pltpu.VMEM((pairs + 1, HH // 4, WW, 2 * width), f32),
            pltpu.VMEM((HH // 4 * (WW // 4), 2 * width), f32),
            pltpu.VMEM((HH // 4 * (WW // 4), 2 * width), f32),
            pltpu.VMEM((n_tm, 2, block // 2, 2 * width), bf16),
            pltpu.VMEM((heads, spans * block, width), bf16),
            pltpu.VMEM((heads, spans * block, width), bf16),
            pltpu.VMEM((n_chan, rows, width), bf16),
            dma((9,)),
            dma((3, pairs, 2)),
            dma((3, pairs, 2)),
            dma((3,)),
            dma((3,)),
            dma,
            dma,
            dma((max(7, 2 * reach), 2)),
            dma((n_tm, 2)),
            dma((3, frames)),
            dma((3, frames)),
        ],
        compiler_params=pltpu.CompilerParams(
            collective_id=0, has_side_effects=True, vmem_limit_bytes=63 * 1024 * 1024
        ),
    )(tokens.reshape(pairs, 2, HH // 4, 4, WW, width), w_query, w_key, w_value, w_out, pool_kernel)


def solution(mesh):
    shape = dict(mesh.shape)
    return jax.shard_map(
        functools.partial(per_device, shape["tm"], shape["chan"]),
        mesh=mesh,
        in_specs=(
            P("tm", "chan"),
            P(None, "chan"),
            P(None, "chan"),
            P(None, "chan"),
            P("chan", None),
            P(),
        ),
        out_specs=P("tm", "chan"),
        check_vma=False,
    )
```
